32 devices in a mesh: row: 8 (over y, x, core), col: 4 (over z).
Axes of the slice: x: 2, y: 2, z: 4, core: 2. Of those that a mesh axis runs over, the one named last changes fastest.
Arguments:
- tokens: bfloat16 [16384, 1088], P(('row', 'col')), may hold values from -6 to 6
- segments: int32 [32, 512], P(('row', 'col')), may hold values from 0 to 3, never falling along the last dimension, each value on 1 to 256 neighbouring positions
- w_qkv: bfloat16 [1088, 3264], P('row', 'col'), may hold values from -0.1875 to 0.1875
- b_query: bfloat16 [1088], P('row'), may hold values from -3 to 3
- b_value: bfloat16 [1088], P('row'), may hold values from -3 to 3
- w_out: bfloat16 [1088, 1088], P('row', 'col'), may hold values from -0.5 to 0.5
- b_out: bfloat16 [1088], P('row'), may hold values from -3 to 3
- w_up: bfloat16 [1088, 4352], P('row', 'col'), may hold values from -0.1875 to 0.1875
- w_down: bfloat16 [4352, 1088], P('row', 'col'), may hold values from -0.09375 to 0.09375
- gain_one: bfloat16 [1088], P('row'), may hold values from 0.25 to 1.75
- gain_two: bfloat16 [1088], P('row'), may hold values from 0.25 to 1.75
- cotangent: bfloat16 [16384, 1088], P(('row', 'col')), may hold values from -6 to 6
Outputs:
- output: float32 [16384, 1088], P(('row', 'col'))
- grad_tokens: float32 [16384, 1088], P(('row', 'col'))
- grad_w_qkv: float32 [1088, 3264], P('row', 'col')
- grad_b_query: float32 [1088], P('row')
- grad_b_value: float32 [1088], P('row')
- grad_w_out: float32 [1088, 1088], P('row', 'col')
- grad_b_out: float32 [1088], P('row')
- grad_w_up: float32 [1088, 4352], P('row', 'col')
- grad_w_down: float32 [4352, 1088], P('row', 'col')
- grad_gain_one: float32 [1088], P('row')
- grad_gain_two: float32 [1088], P('row')
The draws below stay inside these ranges and needn't reach their ends.
Inputs may be any that keep to these rules, and one draw needn't show every extreme that they name: `segments`: in each row of 512 positions the document numbers never fall, and each document spans 1 to 256 positions.
All inputs are finite; a program needn't handle non-finite values.
Results may differ from the reference program's by a relative error of at most 0.015.
Values may be sent and summed in bfloat16 or wider, within the bound.
No kernel may reach another device: no remote copies, remote signals or barrier semaphores. Data moves between devices by JAX's collectives and lax.ppermute only.
A program may use at most 256 MiB of HBM per device.

```python
import math
import jax
import jax.numpy as jnp
import numpy as np
from jax import lax

D = 1088
HEADS = 17
HEAD_DIM = 64
FF = 4352
SEQ_LEN = 512
SEG_COUNT = 4
SEG_MOST = 256
SEQS = 32
TOKENS = 16384


def steps_of(rng, dims, cuts, low, high):
    def one(axis_at, blocks):
        steps = jax.random.uniform(jax.random.fold_in(jax.random.fold_in(rng, 6), axis_at), (blocks,), jnp.float32, low / len(cuts), high / len(cuts))
        return jnp.repeat(jnp.exp(steps), dims[axis_at] // blocks).reshape((-1,) + (1,) * (len(dims) - axis_at - 1))

    gain = one(*cuts[0])
    for cut in cuts[1:]:
        gain = gain * one(*cut)
    return gain


def split_up(number_of, total, reach, slope):
    loads = [(1 << 20) // math.isqrt(grade ** slope) + 1 for grade in range(2, number_of + 1)]
    rest, holding = total - reach - (number_of - 1), [1] * (number_of - 1)
    while rest > 0:
        movable = [i for i in range(number_of - 1) if holding[i] < reach]
        whole, left = sum([loads[i] for i in movable]), rest
        for i in movable:
            addition = min(reach - holding[i], max(1, left * loads[i] // whole), rest)
            holding[i] = holding[i] + addition
            rest = rest - addition
    return np.array([reach] + holding)


def uneven(stream_key, number_of, total, limit, lean):
    if number_of == 2:
        one = jax.random.randint(stream_key, (), max(1, total - limit), min(limit, total - 1) + 1)
        return jnp.stack([one, total - one])
    sizes = jnp.asarray(split_up(number_of, total, limit, lean), jnp.int32)
    twos = (number_of - 1) // 2
    giver, sink = sizes[1:1 + 2 * twos:2], sizes[2:2 + 2 * twos:2]
    margin = jnp.minimum(giver - 1, limit - sink)
    moved = jax.random.randint(jax.random.fold_in(stream_key, 1), (twos,), 0, 1 << 20) % (margin + 1)
    sizes = sizes.at[1:1 + 2 * twos:2].set(giver - moved).at[2:2 + 2 * twos:2].set(sink + moved)
    return sizes[jax.random.permutation(jax.random.fold_in(stream_key, 2), number_of)]


def scatter_about(rng, extent, scale, limit, shards=(), kind=jnp.bfloat16):
    level = steps_of(rng, extent, shards, -0.22, 0.18) if shards else 1.0
    array = jax.random.normal(rng, extent, jnp.float32) * scale * level
    return jnp.minimum(jnp.maximum(array, -limit), limit).astype(kind)


def setup_inputs(seed: int = 0) -> dict:
    keys = jax.random.split(jax.random.key(seed), 13)
    return {
        "tokens": scatter_about(keys[0], (TOKENS, D), 1.0, 6.0, ((0, 32),)),
        "segments": jax.vmap(lambda own: jnp.searchsorted(jnp.cumsum(uneven(own, SEG_COUNT, SEQ_LEN, SEG_MOST, 2)), jnp.arange(SEQ_LEN), side="right"))(jax.random.split(keys[1], SEQS)).reshape((SEQS, SEQ_LEN)).astype(jnp.int32),
        "w_qkv": scatter_about(keys[2], (D, 3 * D), D ** -0.5, 0.1875, ((0, 8), (1, 4))),
        "b_query": scatter_about(keys[3], (D,), 0.5, 3.0, ((0, 8),)),
        "b_value": scatter_about(keys[4], (D,), 0.5, 3.0, ((0, 8),)),
        "w_out": scatter_about(keys[5], (D, D), (D // 8) ** -0.5, 0.5, ((0, 8), (1, 4))),
        "b_out": scatter_about(keys[6], (D,), 0.5, 3.0, ((0, 8),)),
        "w_up": scatter_about(keys[7], (D, FF), D ** -0.5, 0.1875, ((0, 8), (1, 4))),
        "w_down": scatter_about(keys[8], (FF, D), FF ** -0.5, 0.09375, ((0, 8), (1, 4))),
        "gain_one": jnp.clip(1.0 + 0.15 * jax.random.normal(keys[9], (D,), jnp.float32), 0.25, 1.75).astype(jnp.bfloat16),
        "gain_two": jnp.clip(1.0 + 0.15 * jax.random.normal(keys[10], (D,), jnp.float32), 0.25, 1.75).astype(jnp.bfloat16),
        "cotangent": scatter_about(keys[11], (TOKENS, D), 1.0, 6.0, ((0, 32),)),
    }


highest = lax.Precision.HIGHEST
epsilon = 1e-05
big_negative = -1e+30

@jax.custom_vjp
def low(v):
    return lax.optimization_barrier(v.astype(jnp.bfloat16)).astype(jnp.float32)

@jax.custom_vjp
def low_back(v):
    return v

def low_keep(v):
    return (low(v), None)

def low_pass(kept, grad):
    return (grad,)

def back_keep(v):
    return (v, None)

def back_low(kept, grad):
    return (low(grad),)
low.defvjp(low_keep, low_pass)
low_back.defvjp(back_keep, back_low)

def product(left, right):
    return jnp.dot(left, right, precision=highest)

def normalize(values, gain_values):
    average = lax.optimization_barrier(jnp.mean(values, axis=-1, keepdims=True))
    spread = lax.optimization_barrier(jnp.mean(values * values, axis=-1, keepdims=True)) - average * average
    return (values - average) * lax.rsqrt(spread + epsilon) * gain_values

def gelu_tanh(values):
    inner = math.sqrt(2.0 / math.pi) * (values + 0.044715 * values * values * values)
    return 0.5 * values * (1.0 + jnp.tanh(inner))

def attend_one(pieces):
    queries, key_heads, value_heads, segment = pieces
    length = queries.shape[0]
    queries = queries.reshape(length, HEADS, HEAD_DIM)
    key_heads = key_heads.reshape(length, HEADS, HEAD_DIM)
    value_heads = value_heads.reshape(length, HEADS, HEAD_DIM)
    score_scale = 1.0 / math.sqrt(HEAD_DIM)
    scores = low_back(jnp.einsum('qhd,khd->hqk', queries, key_heads, precision=highest) * score_scale)
    positions = jnp.arange(length)
    allowed = (positions[:, None] >= positions[None, :]) & (segment[:, None] == segment[None, :])
    logits = jnp.where(allowed[None], scores, big_negative)
    probabilities = low(jax.nn.softmax(logits, axis=-1))
    mixed_heads = jnp.einsum('hqk,khd->qhd', probabilities, value_heads, precision=highest)
    return mixed_heads.reshape(length, HEADS * HEAD_DIM)

def block_forward(params, inputs, segment_rows):
    w_qkv, b_query, b_value, w_out, b_out, w_up, w_down, gain_one, gain_two = params
    width = inputs.shape[1]
    normed_one = low(normalize(inputs, gain_one))
    bias_all = jnp.concatenate([b_query, jnp.zeros_like(b_query), b_value])
    projected = low(low_back(product(normed_one, w_qkv) + bias_all))
    count = segment_rows.shape[0]
    grouped = projected.reshape(count, SEQ_LEN, 3 * width)
    mixed_heads = lax.map(jax.checkpoint(attend_one), (grouped[:, :, :width], grouped[:, :, width:2 * width], grouped[:, :, 2 * width:], segment_rows))
    mixed_flat = low(low_back(mixed_heads.reshape(-1, width)))
    hidden = inputs + low_back(product(mixed_flat, w_out) + b_out)
    normed_two = low(normalize(hidden, gain_two))
    upward = low_back(product(normed_two, w_up))
    activated = low(gelu_tanh(upward))
    return hidden + low_back(product(activated, w_down))

def reference(tokens, segments, w_qkv, b_query, b_value, w_out, b_out, w_up, w_down, gain_one, gain_two, cotangent):
    params = tuple((member.astype(jnp.float32) for member in (w_qkv, b_query, b_value, w_out, b_out, w_up, w_down, gain_one, gain_two)))
    width = tokens.shape[1]
    seq_count = segments.shape[0]
    group_seqs = math.gcd(seq_count, max(1, 4096 // SEQ_LEN))
    groups = seq_count // group_seqs
    group_rows = group_seqs * SEQ_LEN
    token_groups = tokens.astype(jnp.float32).reshape(groups, group_rows, width)
    upstream_groups = cotangent.astype(jnp.float32).reshape(groups, group_rows, width)
    segment_groups = segments.reshape(groups, group_seqs, SEQ_LEN)

    def one_group(totals, pieces):
        inputs, upstream, segment_rows = pieces

        def forward(params_now, inputs_now):
            return block_forward(params_now, inputs_now, segment_rows)
        result, pullback = jax.vjp(forward, params, inputs)
        grad_params, grad_inputs = pullback(upstream)
        totals = jax.tree.map(jnp.add, totals, grad_params)
        return (totals, (result, grad_inputs))
    initial = jax.tree.map(jnp.zeros_like, params)
    totals, (results, grad_groups) = lax.scan(one_group, initial, (token_groups, upstream_groups, segment_groups))
    output = results.reshape(-1, width)
    grad_tokens = grad_groups.reshape(-1, width)
    return (output, grad_tokens, totals[0], totals[1], totals[2], totals[3], totals[4], totals[5], totals[6], totals[7], totals[8])
```

```python
import math

import jax
import jax.numpy as jnp
from jax import lax
from jax.sharding import PartitionSpec as P

D = 1088
HEADS = 17
HEAD_DIM = 64
SEQ_LEN = 512


epsilon = 1e-05
big_negative = -1e30


def gelu_tanh(values):
    inner = math.sqrt(2.0 / math.pi) * (values + 0.044715 * values * values * values)
    return 0.5 * values * (1.0 + jnp.tanh(inner))


def norm_parts(values):
    average = jnp.mean(values, axis=1, keepdims=True)
    spread = jnp.mean(values * values, axis=1, keepdims=True) - average * average
    inverse = lax.rsqrt(spread + epsilon)
    return ((values - average) * inverse, inverse)


def norm_backward(upstream, centered, inverse, gain_values):
    scaled = upstream * gain_values
    first = jnp.mean(scaled, axis=1, keepdims=True)
    second = jnp.mean(scaled * centered, axis=1, keepdims=True)
    return (inverse * (scaled - first - centered * second), jnp.sum(upstream * centered, axis=0))


def split_heads(packed):
    length = packed.shape[0]
    queries = packed[:, :D].reshape(length, HEADS, HEAD_DIM)
    key_heads = packed[:, D : 2 * D].reshape(length, HEADS, HEAD_DIM)
    value_heads = packed[:, 2 * D :].reshape(length, HEADS, HEAD_DIM)
    return (queries, key_heads, value_heads)


def allowed_pairs(segment):
    positions = jnp.arange(segment.shape[0])
    return (positions[:, None] >= positions[None, :]) & (segment[:, None] == segment[None, :])


def attend_forward(pieces):
    packed, segment = pieces
    queries, key_heads, value_heads = split_heads(packed)
    score_scale = 1.0 / math.sqrt(HEAD_DIM)
    scores = (
        jnp.einsum("qhd,khd->hqk", queries, key_heads, preferred_element_type=jnp.float32)
        * score_scale
    )
    logits = jnp.where(allowed_pairs(segment)[None], scores, big_negative)
    row_peak = jnp.max(logits, axis=2, keepdims=True)
    exponent = jnp.exp(logits - row_peak)
    row_total = jnp.sum(exponent, axis=2, keepdims=True)
    probabilities = (exponent / row_total).astype(jnp.bfloat16)
    mixed_heads = jnp.einsum(
        "hqk,khd->qhd", probabilities, value_heads, preferred_element_type=jnp.float32
    )
    mixed_flat = mixed_heads.reshape(packed.shape[0], D).astype(jnp.bfloat16)
    return (mixed_flat, (row_peak + jnp.log(row_total))[:, :, 0])


def attend_backward(pieces):
    packed, segment, log_totals, grad_mixed = pieces
    length = packed.shape[0]
    queries, key_heads, value_heads = split_heads(packed)
    score_scale = 1.0 / math.sqrt(HEAD_DIM)
    scores = (
        jnp.einsum("qhd,khd->hqk", queries, key_heads, preferred_element_type=jnp.float32)
        * score_scale
    )
    allowed = allowed_pairs(segment)[None]
    probabilities = jnp.where(allowed, jnp.exp(scores - log_totals[:, :, None]), 0.0)
    low_probs = probabilities.astype(jnp.bfloat16)
    grad_heads = grad_mixed.reshape(length, HEADS, HEAD_DIM)
    grad_values = jnp.einsum(
        "hqk,qhd->khd", low_probs, grad_heads, preferred_element_type=jnp.float32
    )
    grad_probs = jnp.einsum(
        "qhd,khd->hqk", grad_heads, value_heads, preferred_element_type=jnp.float32
    )
    row_inner = jnp.sum(grad_probs * probabilities, axis=2, keepdims=True)
    grad_scores = (probabilities * (grad_probs - row_inner)).astype(jnp.bfloat16)
    grad_queries = (
        jnp.einsum("hqk,khd->qhd", grad_scores, key_heads, preferred_element_type=jnp.float32)
        * score_scale
    )
    grad_keys = (
        jnp.einsum("hqk,qhd->khd", grad_scores, queries, preferred_element_type=jnp.float32)
        * score_scale
    )
    joined = jnp.concatenate(
        [
            grad_queries.reshape(length, D),
            grad_keys.reshape(length, D),
            grad_values.reshape(length, D),
        ],
        axis=1,
    )
    return joined.astype(jnp.bfloat16)


def ring_of(chips):
    side = math.isqrt(chips)
    if side * side != chips or side % 2:
        return list(range(chips))
    cells = [(0, x) for x in range(side)]
    for y in range(1, side):
        across = range(side - 1, 0, -1) if y % 2 else range(1, side)
        cells += [(y, x) for x in across]
    cells += [(y, 0) for y in range(side - 1, 0, -1)]
    return [y * side + x for y, x in cells]


class Plane:
    def __init__(self, row_size, col_size):
        self.chips = row_size // 2
        self.cols = col_size
        self.ring = ring_of(self.chips)
        row = lax.axis_index("row")
        self.core = row % 2
        chip = row // 2
        place = [0] * self.chips
        for at, member in enumerate(self.ring):
            place[member] = at
        self.place = jnp.asarray(place, jnp.int32)[chip]
        self.table = jnp.asarray(self.ring, jnp.int32)
        self.z = lax.axis_index("col")

    def chip_at(self, offset):
        return self.table[(self.place + offset) % self.chips]

    def hop(self, value, offset):
        pairs = []
        for at in range(self.chips):
            source, target = self.ring[at], self.ring[(at + offset) % self.chips]
            pairs += [(2 * source + core, 2 * target + core) for core in range(2)]
        return lax.ppermute(value, "row", pairs)

    def swap(self, value):
        pairs = [(place, place ^ 1) for place in range(2 * self.chips)]
        return lax.ppermute(value, "row", pairs)

    def turn(self, value, offset):
        pairs = [(at, (at + offset) % self.cols) for at in range(self.cols)]
        return lax.ppermute(value, "col", pairs)


def half_rows(rows):
    return (rows // 2 + 7) // 8 * 8


def gather_columns(plane, shard):
    pieces = [shard] + [plane.turn(shard, k) for k in range(1, plane.cols)]
    stacked = jnp.stack(pieces)
    blocks = [
        lax.dynamic_index_in_dim(stacked, (plane.z - at) % plane.cols, 0, keepdims=False)
        for at in range(plane.cols)
    ]
    return jnp.concatenate(blocks, axis=1)


def gather_rows(plane, block):
    rows, width = block.shape
    cut = half_rows(rows)
    reach = plane.chips // 2
    found = [(0, 0, block)]
    ahead = behind = block
    for step in range(1, reach):
        ahead, behind = plane.hop(ahead, 1), plane.hop(behind, -1)
        found += [(-step, 0, ahead), (step, 0, behind)]
    found.append((reach, 0, plane.hop(ahead[:cut], 1)))
    found.append((reach, cut, plane.hop(behind[cut:], -1)))
    whole = jnp.zeros((plane.chips, 2, rows, width), block.dtype)
    for offset, row_at, piece in found:
        chip = plane.chip_at(offset)
        whole = lax.dynamic_update_slice(whole, piece[None, None], (chip, plane.core, row_at, 0))
        whole = lax.dynamic_update_slice(
            whole, plane.swap(piece)[None, None], (chip, 1 - plane.core, row_at, 0)
        )
    return whole.reshape(plane.chips * 2 * rows, width)


def scatter_rows(plane, partial):
    rows = partial.shape[0] // (2 * plane.chips)
    width = partial.shape[1]
    split = partial.reshape(plane.chips, 2, rows, width)
    theirs = lax.dynamic_index_in_dim(split, 1 - plane.core, 1, keepdims=False)
    mine = lax.dynamic_index_in_dim(split, plane.core, 1, keepdims=False)
    both = add_low(mine, plane.swap(theirs))

    def term(offset):
        return lax.dynamic_index_in_dim(both, plane.chip_at(offset), 0, keepdims=False)

    cut = half_rows(rows)
    reach = plane.chips // 2
    far = term(reach)
    ahead, behind = plane.hop(far[:cut], 1), plane.hop(far[cut:], -1)
    for step in range(2, reach + 1):
        near_ahead, near_behind = term(reach - step + 1), term(-(reach - step + 1))
        if step == 2:
            near_ahead = jnp.concatenate([add_low(near_ahead[:cut], ahead), near_ahead[cut:]])
            near_behind = jnp.concatenate([near_behind[:cut], add_low(near_behind[cut:], behind)])
        else:
            near_ahead, near_behind = add_low(near_ahead, ahead), add_low(near_behind, behind)
        ahead, behind = plane.hop(near_ahead, 1), plane.hop(near_behind, -1)
    own = term(0).astype(jnp.float32)
    return (own + ahead.astype(jnp.float32) + behind.astype(jnp.float32)).astype(jnp.bfloat16)


def add_low(left, right):
    return (left.astype(jnp.float32) + right.astype(jnp.float32)).astype(jnp.bfloat16)


def scatter_columns(plane, block):
    width = block.shape[1] // plane.cols
    stacked = jnp.stack([block[:, at * width : (at + 1) * width] for at in range(plane.cols)])

    def part(offset):
        return lax.dynamic_index_in_dim(stacked, (plane.z + offset) % plane.cols, 0, keepdims=False)

    total = part(0).astype(jnp.float32)
    for k in range(1, plane.cols):
        total = total + plane.turn(part(k), k).astype(jnp.float32)
    return total


def gather_vectors(plane, packed):
    count, rows = packed.shape
    whole = jnp.zeros((plane.chips, 2, count, rows), packed.dtype)
    for offset in range(plane.chips):
        piece = plane.hop(packed, offset) if offset else packed
        chip = plane.chip_at(-offset)
        whole = lax.dynamic_update_slice(whole, piece[None, None], (chip, plane.core, 0, 0))
        whole = lax.dynamic_update_slice(
            whole, plane.swap(piece)[None, None], (chip, 1 - plane.core, 0, 0)
        )
    return whole.transpose(2, 0, 1, 3).reshape(count, plane.chips * 2 * rows)


def sum_everywhere(plane, value):
    value = value + plane.swap(value)
    value = sum([plane.hop(value, k) for k in range(1, plane.chips)], value)
    return sum([plane.turn(value, k) for k in range(1, plane.cols)], value)


def local(
    tokens,
    segments,
    w_qkv,
    b_query,
    b_value,
    w_out,
    b_out,
    w_up,
    w_down,
    gain_one,
    gain_two,
    cotangent,
):
    plane = Plane(lax.axis_size("row"), lax.axis_size("col"))
    blank = jnp.zeros_like(b_query)
    packed = jnp.stack([b_query, b_value, b_out, gain_one, gain_two, blank, blank, blank])
    vectors = gather_vectors(plane, packed).astype(jnp.float32)
    bias_query, bias_value, bias_out, gain_first, gain_second = (vectors[at] for at in range(5))
    qkv_full = gather_rows(plane, gather_columns(plane, w_qkv))
    out_full = gather_rows(plane, gather_columns(plane, w_out))
    up_full = gather_rows(plane, gather_columns(plane, w_up))
    down_full = gather_rows(plane, gather_columns(plane, w_down))

    def weight_gradient(left, right):
        product = jnp.einsum("ta,tb->ab", left, right, preferred_element_type=jnp.float32)
        block = scatter_rows(plane, product.astype(jnp.bfloat16))
        return scatter_columns(plane, block)

    inputs = tokens.astype(jnp.float32)
    centered_one, inverse_one = norm_parts(inputs)
    normed_one = (centered_one * gain_first).astype(jnp.bfloat16)
    bias_all = jnp.concatenate([bias_query, jnp.zeros_like(bias_query), bias_value])
    projected = (
        jnp.dot(normed_one, qkv_full, preferred_element_type=jnp.float32) + bias_all
    ).astype(jnp.bfloat16)
    grouped = projected.reshape(-1, SEQ_LEN, 3 * D)
    mixed_seqs, log_totals = lax.map(attend_forward, (grouped, segments))
    mixed_flat = mixed_seqs.reshape(-1, D)
    hidden = (
        inputs + jnp.dot(mixed_flat, out_full, preferred_element_type=jnp.float32) + bias_out
    )
    centered_two, inverse_two = norm_parts(hidden)
    normed_two = (centered_two * gain_second).astype(jnp.bfloat16)
    upward = jnp.dot(normed_two, up_full, preferred_element_type=jnp.float32)
    activated, gelu_back = jax.vjp(gelu_tanh, upward)
    activated_low = activated.astype(jnp.bfloat16)
    grad_w_down = weight_gradient(activated_low, cotangent)
    output = hidden + jnp.dot(activated_low, down_full, preferred_element_type=jnp.float32)
    grad_activated = jnp.einsum(
        "td,fd->tf", cotangent, down_full, preferred_element_type=jnp.float32
    )
    grad_upward = gelu_back(grad_activated)[0].astype(jnp.bfloat16)
    grad_w_up = weight_gradient(normed_two, grad_upward)
    grad_normed_two = jnp.einsum(
        "tf,df->td", grad_upward, up_full, preferred_element_type=jnp.float32
    )
    grad_hidden_norm, gain_two_terms = norm_backward(
        grad_normed_two, centered_two, inverse_two, gain_second
    )
    grad_hidden = cotangent.astype(jnp.float32) + grad_hidden_norm
    grad_branch = grad_hidden.astype(jnp.bfloat16)
    grad_w_out = weight_gradient(mixed_flat, grad_branch)
    grad_mixed = jnp.einsum(
        "td,cd->tc", grad_branch, out_full, preferred_element_type=jnp.float32
    ).astype(jnp.bfloat16)
    grad_seqs = lax.map(
        attend_backward, (grouped, segments, log_totals, grad_mixed.reshape(-1, SEQ_LEN, D))
    )
    grad_projected = grad_seqs.reshape(-1, 3 * D)
    grad_w_qkv = weight_gradient(normed_one, grad_projected)
    grad_normed_one = jnp.einsum(
        "tf,df->td", grad_projected, qkv_full, preferred_element_type=jnp.float32
    )
    grad_input_norm, gain_one_terms = norm_backward(
        grad_normed_one, centered_one, inverse_one, gain_first
    )
    grad_tokens = grad_hidden + grad_input_norm
    bias_terms = jnp.sum(grad_projected.astype(jnp.float32), axis=0)
    out_terms = jnp.sum(grad_branch.astype(jnp.float32), axis=0)
    nothing = jnp.zeros_like(out_terms)
    sums = sum_everywhere(
        plane,
        jnp.stack(
            [
                bias_terms[:D],
                bias_terms[2 * D :],
                out_terms,
                gain_one_terms,
                gain_two_terms,
                nothing,
                nothing,
                nothing,
            ]
        ),
    )
    stretch_size = D // lax.axis_size("row")
    own = lax.dynamic_index_in_dim(
        sums.reshape(8, -1, stretch_size), lax.axis_index("row"), 1, keepdims=False
    )
    return (
        output,
        grad_tokens,
        grad_w_qkv,
        own[0],
        own[1],
        grad_w_out,
        own[2],
        grad_w_up,
        grad_w_down,
        own[3],
        own[4],
    )


def solution(mesh):
    in_specs = (
        P(("row", "col"), None),
        P(("row", "col"), None),
        P("row", "col"),
        P("row"),
        P("row"),
        P("row", "col"),
        P("row"),
        P("row", "col"),
        P("row", "col"),
        P("row"),
        P("row"),
        P(("row", "col"), None),
    )
    out_specs = (
        P(("row", "col"), None),
        P(("row", "col"), None),
        P("row", "col"),
        P("row"),
        P("row"),
        P("row", "col"),
        P("row"),
        P("row", "col"),
        P("row", "col"),
        P("row"),
        P("row"),
    )
    return jax.shard_map(local, mesh=mesh, in_specs=in_specs, out_specs=out_specs, check_vma=False)
```
